32 devices in a mesh: section: 2 (over y), fsdp: 4 (over x, core), replica: 4 (over z).
Axes of the slice: x: 2, y: 2, z: 4, core: 2. Of those that a mesh axis runs over, the one named last changes fastest.
Arguments:
- images: bfloat16 [4, 32, 14, 14, 512], P(None, ('fsdp', 'replica')), may hold values from -6 to 6
- cotangent: bfloat16 [4, 32, 14, 14, 512], P(None, ('fsdp', 'replica')), may hold values from -6 to 6
- counts: int32 [4, 16], P(None, ('fsdp', 'replica')), may hold values from 1 to 2, as said below
- regions: int32 [14, 14], replicated, may hold values from 0 to 8, as said below
- relpos: int32 [49, 49], replicated, may hold values from 0 to 168, as said below
- qkv_weight: bfloat16 [2, 512, 1536], P('section', 'fsdp'), may hold values from -0.25 to 0.25
- proj_weight: bfloat16 [2, 512, 512], P('section', 'fsdp'), may hold values from -1.5 to 1.5
- fc1_weight: bfloat16 [2, 512, 2048], P('section', 'fsdp'), may hold values from -0.25 to 0.25
- fc2_weight: bfloat16 [2, 2048, 512], P('section', 'fsdp'), may hold values from -0.125 to 0.125
- gains: bfloat16 [2, 2, 512], P('section', None, 'fsdp'), may hold values from 0.099609375 to 1.8984375
- biases: bfloat16 [2, 6, 512], P('section', None, 'fsdp'), may hold values from -3 to 3
- fc1_bias: bfloat16 [2, 2048], P('section', 'fsdp'), may hold values from -3 to 3
- rel_table: bfloat16 [2, 169, 16], P('section', None, 'fsdp'), may hold values from -5 to 5
Outputs:
- block_out: bfloat16 [2, 4, 32, 14, 14, 512], P('section', None, ('fsdp', 'replica'))
- input_grad: float32 [2, 4, 32, 14, 14, 512], P('section', None, ('fsdp', 'replica'))
- grad_qkv: float32 [2, 512, 1536], P('section', 'fsdp')
- grad_proj: float32 [2, 512, 512], P('section', 'fsdp')
- grad_fc1: float32 [2, 512, 2048], P('section', 'fsdp')
- grad_fc2: float32 [2, 2048, 512], P('section', 'fsdp')
- grad_gains: float32 [2, 2, 512], P('section', None, 'fsdp')
- grad_biases: float32 [2, 6, 512], P('section', None, 'fsdp')
- grad_fc1_bias: float32 [2, 2048], P('section', 'fsdp')
- grad_table: float32 [2, 169, 16], P('section', None, 'fsdp')
The draws below stay inside these ranges and needn't reach their ends.
Inputs may be any that keep to these rules, and one draw needn't show every extreme that they name: `counts`: slots 0 to count - 1 of a device's 2 slots in a micro-batch are live; in every micro-batch some device has all 2 live. `regions`: region ids are constant on bands: id = 3 * band(row) + band(column) with the same two cut positions for rows and columns. `relpos`: pairs with the same relative offset share a row; every row is used.
All inputs are finite; a program needn't handle non-finite values.
Results may differ from the reference program's by a relative error of at most 0.019.
Values may be sent and summed in bfloat16 or wider, within the bound.
No kernel may reach another device: no remote copies, remote signals or barrier semaphores. Data moves between devices by JAX's collectives and lax.ppermute only.
A program may use at most 320 MiB of HBM per device.

```python
import jax
import jax.numpy as jnp
from jax import lax

DIM = 512
HEADS = 16
HEAD_DIM = 32
HIDDEN_SIZE = 2048
WIN = 7
SIDE = 14
SHIFT = 3
MICRO = 4
SLOTS = 2
TABLE = 169
GROUPS = 16
IMAGES_MB = 32


def draw_counts(key, part):
    keys = jax.random.split(key, 3)
    wide = jax.random.randint(keys[0], (MICRO, GROUPS), 1, SLOTS + 1)
    coin = jax.random.randint(keys[1], (MICRO, GROUPS), 0, 2)
    base = jnp.where(coin == 0, 1, wide)
    fullest = jax.random.randint(keys[2], (MICRO,), 0, GROUPS)
    column = lax.broadcasted_iota(jnp.int32, (MICRO, GROUPS), 1)
    return jnp.where(column == fullest[:, None], SLOTS, base).astype(jnp.int32)


def draw_regions(key, part):
    keys = jax.random.split(key, 2)
    first_cut = jax.random.randint(keys[0], (), 4, 10)
    second_cut = jax.random.randint(keys[1], (), first_cut + 1, SIDE)
    line = jnp.arange(SIDE, dtype=jnp.int32)
    band = (line >= first_cut).astype(jnp.int32) + (line >= second_cut).astype(jnp.int32)
    return (3 * band[:, None] + band[None, :]).astype(jnp.int32)


def draw_relpos(key, part):
    order = jax.random.permutation(key, TABLE).astype(jnp.int32)
    cell = jnp.arange(WIN * WIN, dtype=jnp.int32)
    row_of = cell // WIN
    col_of = cell % WIN
    offsets = (row_of[:, None] - row_of[None, :] + WIN - 1) * (2 * WIN - 1) + (col_of[:, None] - col_of[None, :] + WIN - 1)
    return order[offsets].astype(jnp.int32)


def level_of(stream_key, extent, pieces, least, high):
    def one(position, blocks):
        draws = jax.random.uniform(jax.random.fold_in(jax.random.fold_in(stream_key, 6), position), (blocks,), jnp.float32, least / len(pieces), high / len(pieces))
        return jnp.repeat(jnp.exp(draws), extent[position] // blocks).reshape((-1,) + (1,) * (len(extent) - position - 1))

    loudness = one(*pieces[0])
    for cut in pieces[1:]:
        loudness = loudness * one(*cut)
    return loudness


def gaussian(stream_key, extent, deviation, bound, cuts=(), kind=jnp.bfloat16):
    drawn = deviation * jax.random.normal(stream_key, extent, jnp.float32)
    if cuts:
        drawn = drawn * level_of(stream_key, extent, cuts, -0.22, 0.18)
    return jnp.clip(drawn, -bound, bound).astype(kind)


def setup_inputs(seed: int = 0) -> dict:
    streams_of = jax.random.split(jax.random.key(seed), 14)
    images = gaussian(streams_of[0], (MICRO, IMAGES_MB, SIDE, SIDE, DIM), 1.0, 6.0, ((1, 16),))
    cotangent = gaussian(streams_of[1], (MICRO, IMAGES_MB, SIDE, SIDE, DIM), 1.0, 6.0, ((1, 16),))
    counts = draw_counts(jax.random.fold_in(streams_of[13], 71), 0)
    regions = draw_regions(jax.random.fold_in(streams_of[13], 71), 0)
    relpos = draw_relpos(jax.random.fold_in(streams_of[13], 71), 0)
    qkv_weight = gaussian(streams_of[5], (2, DIM, 3 * DIM), DIM ** -0.5, 0.25, ((0, 2), (1, 4)))
    proj_weight = gaussian(streams_of[6], (2, DIM, DIM), (DIM // 32) ** -0.5, 1.5, ((0, 2), (1, 4)))
    fc1_weight = gaussian(streams_of[7], (2, DIM, HIDDEN_SIZE), DIM ** -0.5, 0.25, ((0, 2), (1, 4)))
    fc2_weight = gaussian(streams_of[8], (2, HIDDEN_SIZE, DIM), HIDDEN_SIZE ** -0.5, 0.125, ((0, 2), (1, 4)))
    gains = jnp.clip(1.0 + 0.18 * jax.random.normal(streams_of[9], (2, 2, DIM), jnp.float32), 0.099609375, 1.8984375).astype(jnp.bfloat16)
    biases = gaussian(streams_of[10], (2, 6, DIM), 0.5, 3.0, ((0, 2), (2, 4)))
    fc1_bias = gaussian(streams_of[11], (2, HIDDEN_SIZE), 0.5, 3.0, ((0, 2), (1, 4)))
    rel_table = gaussian(streams_of[12], (2, TABLE, HEADS), 1.0, 5.0, ((0, 2), (2, 4)))
    return {"images": images, "cotangent": cotangent, "counts": counts, "regions": regions, "relpos": relpos, "qkv_weight": qkv_weight, "proj_weight": proj_weight, "fc1_weight": fc1_weight, "fc2_weight": fc2_weight, "gains": gains, "biases": biases, "fc1_bias": fc1_bias, "rel_table": rel_table}


EPSILON = 1e-05
ROOT_HALF = 0.7071067811865476
INV_ROOT_TAU = 0.3989422804014327

def layer_norm(values, gain, offset_row):
    center = values - lax.optimization_barrier(jnp.mean(values, axis=-1, keepdims=True))
    spread = lax.optimization_barrier(jnp.mean(center * center, axis=-1, keepdims=True))
    scaled = lax.rsqrt(spread + EPSILON)
    normed = center * scaled
    return (normed * gain + offset_row, normed, scaled)

def norm_backward(upstream, normed, scaled, gain):
    direct = upstream * gain
    return (direct - lax.optimization_barrier(jnp.mean(direct, axis=-1, keepdims=True)) - normed * lax.optimization_barrier(jnp.mean(direct * normed, axis=-1, keepdims=True))) * scaled

def gelu_value(before):
    return 0.5 * before * (1.0 + jax.scipy.special.erf(before * ROOT_HALF))

def gelu_slope(before):
    return 0.5 * (1.0 + jax.scipy.special.erf(before * ROOT_HALF)) + before * INV_ROOT_TAU * jnp.exp(-0.5 * before * before)

def inner_rows(left, right):
    return jnp.dot(left.T, right, preferred_element_type=jnp.float32)

def outer_cols(left, right):
    return jnp.dot(left, right.T, preferred_element_type=jnp.float32)

def to_windows(image_rows, offset):
    rolled = jnp.roll(image_rows, (-offset, -offset), axis=(1, 2))
    count = image_rows.shape[0]
    parts = SIDE // WIN
    shaped = rolled.reshape(count, parts, WIN, parts, WIN, DIM).transpose(0, 1, 3, 2, 4, 5)
    return shaped.reshape(count * SIDE * SIDE, DIM)

def from_windows(window_rows, offset):
    count = window_rows.shape[0] // (SIDE * SIDE)
    parts = SIDE // WIN
    shaped = window_rows.reshape(count, parts, parts, WIN, WIN, DIM).transpose(0, 1, 3, 2, 4, 5)
    return jnp.roll(shaped.reshape(count, SIDE, SIDE, DIM), (offset, offset), axis=(1, 2))

def relation_onehot(relpos):
    flat = relpos.reshape(-1)
    return (flat[:, None] == jnp.arange(TABLE, dtype=jnp.int32)[None, :]).astype(jnp.float32)

def region_mask(regions):
    parts = SIDE // WIN
    tiles = regions.reshape(parts, WIN, parts, WIN).transpose(0, 2, 1, 3).reshape(parts * parts, WIN * WIN)
    differ = tiles[:, :, None] != tiles[:, None, :]
    return jnp.where(differ, jnp.float32(-100.0), jnp.float32(0.0))

def attention_add(table, onehot, masking):
    lookup = jnp.dot(onehot, table.astype(jnp.float32), precision=lax.Precision.HIGHEST)
    lookup = lookup.reshape(WIN * WIN, WIN * WIN, HEADS).transpose(2, 0, 1)
    return lookup[None] + masking[:, None]

def forward(rows, params, added):
    qkv_w, proj_w, fc1_w, fc2_w, gain_rows, bias_rows, fc1_b, table = params
    gains_f = gain_rows.astype(jnp.float32)
    biases_f = bias_rows.astype(jnp.float32)
    factor = HEAD_DIM ** (-0.5)
    base = rows.astype(jnp.float32)
    first, normed_a, scaled_a = layer_norm(base, gains_f[0], biases_f[0])
    first_b = first.astype(jnp.bfloat16)
    mixed = jnp.dot(first_b, qkv_w, preferred_element_type=jnp.float32)
    count = rows.shape[0] // (SIDE * SIDE)
    blocks = (count, (SIDE // WIN) ** 2, WIN * WIN, HEADS, HEAD_DIM)
    query_blocks = ((mixed[:, :DIM] + biases_f[1]) * factor).astype(jnp.bfloat16).reshape(blocks)
    key_blocks = mixed[:, DIM:2 * DIM].astype(jnp.bfloat16).reshape(blocks)
    value_blocks = (mixed[:, 2 * DIM:] + biases_f[2]).astype(jnp.bfloat16).reshape(blocks)
    scores = jnp.einsum('swihd,swjhd->swhij', query_blocks.astype(jnp.float32), key_blocks.astype(jnp.float32)) + added[None]
    expo = jnp.exp(scores)
    probs = expo / lax.optimization_barrier(jnp.sum(expo, axis=-1, keepdims=True))
    probs_b = probs.astype(jnp.bfloat16)
    attended = jnp.einsum('swhij,swjhd->swihd', probs_b.astype(jnp.float32), value_blocks.astype(jnp.float32))
    attended = attended.astype(jnp.bfloat16).reshape(rows.shape[0], DIM)
    middle = base + jnp.dot(attended, proj_w, preferred_element_type=jnp.float32) + biases_f[3]
    second, normed_b, scaled_b = layer_norm(middle, gains_f[1], biases_f[4])
    second_b = second.astype(jnp.bfloat16)
    before = jnp.dot(second_b, fc1_w, preferred_element_type=jnp.float32) + fc1_b.astype(jnp.float32)
    hidden_b = gelu_value(before).astype(jnp.bfloat16)
    output = middle + jnp.dot(hidden_b, fc2_w, preferred_element_type=jnp.float32) + biases_f[5]
    saved = (normed_a, scaled_a, first_b, query_blocks, key_blocks, value_blocks, probs, probs_b, attended, normed_b, scaled_b, second_b, before, hidden_b)
    return (output.astype(jnp.bfloat16), saved)

def backward(upstream_rows, saved, params, onehot):
    qkv_w, proj_w, fc1_w, fc2_w, gain_rows, bias_rows, fc1_b, table = params
    gains_f = gain_rows.astype(jnp.float32)
    factor = HEAD_DIM ** (-0.5)
    normed_a, scaled_a, first_b, query_blocks, key_blocks, value_blocks, probs, probs_b, attended, normed_b, scaled_b, second_b, before, hidden_b = saved
    upstream = upstream_rows.astype(jnp.float32)
    grad_fc2_bias = lax.optimization_barrier(jnp.sum(upstream, axis=0))
    grad_fc2 = inner_rows(hidden_b, upstream_rows)
    grad_before = outer_cols(upstream_rows, fc2_w) * gelu_slope(before)
    grad_before_b = grad_before.astype(jnp.bfloat16)
    grad_fc1_bias = lax.optimization_barrier(jnp.sum(grad_before, axis=0))
    grad_fc1 = inner_rows(second_b, grad_before_b)
    grad_second = outer_cols(grad_before_b, fc1_w)
    grad_gain_b = lax.optimization_barrier(jnp.sum(grad_second * normed_b, axis=0))
    grad_shift_b = lax.optimization_barrier(jnp.sum(grad_second, axis=0))
    grad_middle = upstream + norm_backward(grad_second, normed_b, scaled_b, gains_f[1])
    grad_middle_b = grad_middle.astype(jnp.bfloat16)
    grad_proj_bias = lax.optimization_barrier(jnp.sum(grad_middle, axis=0))
    grad_proj = inner_rows(attended, grad_middle_b)
    grad_attended = outer_cols(grad_middle_b, proj_w).astype(jnp.bfloat16).reshape(query_blocks.shape)
    grad_probs = jnp.einsum('swihd,swjhd->swhij', grad_attended.astype(jnp.float32), value_blocks.astype(jnp.float32))
    grad_scores = probs * (grad_probs - lax.optimization_barrier(jnp.sum(probs * grad_probs, axis=-1, keepdims=True)))
    grad_scores_b = grad_scores.astype(jnp.bfloat16).astype(jnp.float32)
    table_terms = lax.optimization_barrier(jnp.sum(grad_scores, axis=(0, 1))).transpose(1, 2, 0).reshape(WIN ** 4, HEADS)
    grad_table = jnp.dot(onehot.T, table_terms, precision=lax.Precision.HIGHEST)
    total_rows = first_b.shape[0]
    grad_queries = (jnp.einsum('swhij,swjhd->swihd', grad_scores_b, key_blocks.astype(jnp.float32)) * factor).reshape(total_rows, DIM)
    grad_keys = jnp.einsum('swhij,swihd->swjhd', grad_scores_b, query_blocks.astype(jnp.float32)).reshape(total_rows, DIM)
    grad_values = jnp.einsum('swhij,swihd->swjhd', probs_b.astype(jnp.float32), grad_attended.astype(jnp.float32)).reshape(total_rows, DIM)
    grad_mixed_b = jnp.concatenate([grad_queries, grad_keys, grad_values], axis=1).astype(jnp.bfloat16)
    grad_qkv = inner_rows(first_b, grad_mixed_b)
    grad_first = outer_cols(grad_mixed_b, qkv_w)
    grad_gain_a = lax.optimization_barrier(jnp.sum(grad_first * normed_a, axis=0))
    grad_shift_a = lax.optimization_barrier(jnp.sum(grad_first, axis=0))
    grad_rows = grad_middle + norm_backward(grad_first, normed_a, scaled_a, gains_f[0])
    grad_gains = jnp.stack([grad_gain_a, grad_gain_b])
    grad_biases = jnp.stack([grad_shift_a, lax.optimization_barrier(jnp.sum(grad_queries, axis=0)), lax.optimization_barrier(jnp.sum(grad_values, axis=0)), grad_proj_bias, grad_shift_b, grad_fc2_bias])
    return (grad_rows, (grad_qkv, grad_proj, grad_fc1, grad_fc2, grad_gains, grad_biases, grad_fc1_bias, grad_table))

def reference(images, cotangent, counts, regions, relpos, qkv_weight, proj_weight, fc1_weight, fc2_weight, gains, biases, fc1_bias, rel_table):
    onehot = relation_onehot(relpos)
    slot_ids = jnp.arange(IMAGES_MB, dtype=jnp.int32) % SLOTS
    live = slot_ids[None, :] < jnp.repeat(counts, SLOTS, axis=1)
    arrays = (qkv_weight, proj_weight, fc1_weight, fc2_weight, gains, biases, fc1_bias, rel_table)
    params = [tuple((item[section_index] for item in arrays)) for section_index in range(2)]
    parts = (SIDE // WIN) ** 2
    adds = [attention_add(params[0][7], onehot, jnp.zeros((parts, WIN * WIN, WIN * WIN), jnp.float32)), attention_add(params[1][7], onehot, region_mask(regions))]
    zero_half = jnp.zeros((), jnp.bfloat16)
    outs_first, outs_second, grads_first, grads_second = ([], [], [], [])
    totals_first, totals_second = (None, None)
    for micro_index in range(MICRO):
        alive = live[micro_index][:, None, None, None]
        rows_a, saved_a = forward(to_windows(images[micro_index], 0), params[0], adds[0])
        middle_out = jnp.where(alive, from_windows(rows_a, 0), zero_half)
        rows_b, saved_b = forward(to_windows(middle_out, SHIFT), params[1], adds[1])
        final_out = jnp.where(alive, from_windows(rows_b, SHIFT), zero_half)
        upstream = jnp.where(alive, cotangent[micro_index], zero_half)
        back_b, terms_b = backward(to_windows(upstream, SHIFT), saved_b, params[1], onehot)
        grad_mid = from_windows(back_b, SHIFT)
        upstream_a = jnp.where(alive, grad_mid.astype(jnp.bfloat16), zero_half)
        back_a, terms_a = backward(to_windows(upstream_a, 0), saved_a, params[0], onehot)
        outs_first.append(middle_out)
        outs_second.append(final_out)
        grads_first.append(from_windows(back_a, 0))
        grads_second.append(grad_mid)
        totals_first = terms_a if totals_first is None else jax.tree.map(lambda left, right: left + right, totals_first, terms_a)
        totals_second = terms_b if totals_second is None else jax.tree.map(lambda left, right: left + right, totals_second, terms_b)
    block_out = jnp.stack([jnp.stack(outs_first), jnp.stack(outs_second)])
    input_grad = jnp.stack([jnp.stack(grads_first), jnp.stack(grads_second)])
    stacked = [jnp.stack([totals_first[index], totals_second[index]]) for index in range(8)]
    return (block_out, input_grad, stacked[0], stacked[1], stacked[2], stacked[3], stacked[4], stacked[5], stacked[6], stacked[7])
```

```python
import jax
import jax.numpy as jnp
from jax import lax
from jax.experimental import pallas as pl
from jax.experimental.pallas import tpu as pltpu
from jax.sharding import PartitionSpec as P

DIM = 512
HEADS = 16
HEAD_DIM = 32
HIDDEN = 2048
WIN = 7
SIDE = 14
SHIFT = 3
TABLE = 169

AREA = WIN * WIN
PARTS = (SIDE // WIN) ** 2
SPAN = 64
ROWS = PARTS * SPAN
LINE = 16
FLAT = SIDE * LINE
GROUP = 8
GROUPS = HEADS // GROUP
KEYS = GROUP * SPAN
FEAT = GROUP * HEAD_DIM
CHUNK = 512
CHUNKS = HIDDEN // CHUNK
SUMS = 16

EPSILON = 1e-05
ROOT_HALF = 0.7071067811865476
INV_ROOT_TAU = 0.3989422804014327
FACTOR = HEAD_DIM ** (-0.5)
NEVER = -1e30

BF = jnp.bfloat16
F32 = jnp.float32


def nn(left, right):
    return lax.dot_general(left, right, (((1,), (0,)), ((), ())), preferred_element_type=F32)


def nt(left, right):
    return lax.dot_general(left, right, (((1,), (1,)), ((), ())), preferred_element_type=F32)


def tn(left, right):
    return lax.dot_general(left, right, (((0,), (0,)), ((), ())), preferred_element_type=F32)


def normalize(values):
    center = values - jnp.mean(values, axis=-1, keepdims=True)
    spread = jnp.mean(center * center, axis=-1, keepdims=True)
    scaled = lax.rsqrt(spread + EPSILON)
    return center * scaled, scaled


def norm_backward(direct, normed, scaled):
    return (
        direct
        - jnp.mean(direct, axis=-1, keepdims=True)
        - normed * jnp.mean(direct * normed, axis=-1, keepdims=True)
    ) * scaled


def fold_heads(stacked, own):
    kept = stacked * own
    total = kept[:SPAN]
    for head in range(1, GROUP):
        total = total + kept[head * SPAN : (head + 1) * SPAN]
    return total


def spread_heads(rows, own):
    return jnp.concatenate([rows] * GROUP, axis=0) * own


def load_image(first_ref, second_ref, later, flat_ref):
    @pl.when(later == 0)
    def _():
        for row in range(SIDE):
            flat_ref[row * LINE : row * LINE + SIDE, :] = first_ref[0, 0, row]

    @pl.when(later != 0)
    def _():
        for row in range(SIDE):
            flat_ref[row * LINE : row * LINE + SIDE, :] = second_ref[0, 0, row]


def forward_kernel(
    info,
    images_ref,
    carried_ref,
    perm_ref,
    back_ref,
    added_ref,
    own_ref,
    same_ref,
    qkv_ref,
    proj_ref,
    fc1_ref,
    fc2_ref,
    rows_ref,
    hidden_ref,
    *rest,
):
    (out_ref, send_ref, n1_ref, h1_ref, scale_ref, mix_ref, p_ref, o_ref, n2_ref, h2_ref, u_ref, slope_ref) = rest[-13:-1]
    flat_ref = rest[-1]
    slot = pl.program_id(0)

    @pl.when(slot == 0)
    def _():
        flat_ref[...] = jnp.zeros_like(flat_ref)

    load_image(images_ref, carried_ref, info[1], flat_ref)
    base = nn(perm_ref[...], flat_ref[...])
    normed_a, scaled_a = normalize(base)
    n1_ref[0, 0] = normed_a.astype(BF)
    first = (normed_a * rows_ref[0:1, :] + rows_ref[2:3, :]).astype(BF)
    h1_ref[0, 0] = first
    scale_ref[0, 0, :, 0:128] = jnp.broadcast_to(scaled_a, (ROWS, 128))
    query = ((nn(first, qkv_ref[:, :DIM]) + rows_ref[3:4, :]) * FACTOR).astype(BF)
    mix_ref[0, 0, :, :DIM] = query
    key = nn(first, qkv_ref[:, DIM : 2 * DIM]).astype(BF)
    mix_ref[0, 0, :, DIM : 2 * DIM] = key
    value = (nn(first, qkv_ref[:, 2 * DIM :]) + rows_ref[4:5, :]).astype(BF)
    mix_ref[0, 0, :, 2 * DIM :] = value
    own = own_ref[...]
    same = same_ref[...]
    for window in range(PARTS):
        at = slice(window * SPAN, (window + 1) * SPAN)
        for group in range(GROUPS):
            feats = slice(group * FEAT, (group + 1) * FEAT)
            keys = slice(group * KEYS, (group + 1) * KEYS)
            scores = nt(query[at, feats], spread_heads(key[at, feats], own)) + added_ref[window, :, keys]
            expo = jnp.exp(scores)
            total = nn(expo.astype(BF), same)
            probs = (expo / total).astype(BF)
            p_ref[0, 0, at, keys] = probs
            o_ref[0, 0, at, feats] = nn(probs, spread_heads(value[at, feats], own)).astype(BF)
    middle = base + nn(o_ref[0, 0], proj_ref[...]) + rows_ref[5:6, :]
    normed_b, scaled_b = normalize(middle)
    n2_ref[0, 0] = normed_b.astype(BF)
    scale_ref[0, 0, :, 128:256] = jnp.broadcast_to(scaled_b, (ROWS, 128))
    second = (normed_b * rows_ref[1:2, :] + rows_ref[6:7, :]).astype(BF)
    h2_ref[0, 0] = second
    output = middle + rows_ref[7:8, :]
    for chunk in range(CHUNKS):
        cols = slice(chunk * CHUNK, (chunk + 1) * CHUNK)
        before = nn(second, fc1_ref[:, cols]) + hidden_ref[0:1, cols]
        share = 0.5 * (1.0 + lax.erf(before * ROOT_HALF))
        hidden = (before * share).astype(BF)
        u_ref[0, 0, :, cols] = hidden
        slope_ref[0, 0, :, cols] = (
            share + before * INV_ROOT_TAU * jnp.exp(-0.5 * before * before)
        ).astype(BF)
        output = output + nn(hidden, fc2_ref[cols, :])
    alive = (slot < info[2]).astype(F32)
    image = (nn(back_ref[...], output.astype(BF)) * alive).astype(BF)
    for row in range(SIDE):
        line = image[row * LINE : row * LINE + SIDE]
        out_ref[0, 0, row] = line
        send_ref[0, 0, row] = line


def backward_kernel(
    info,
    cotangent_ref,
    returned_ref,
    perm_ref,
    back_ref,
    own_ref,
    match_ref,
    qkv_ref,
    proj_ref,
    fc1_ref,
    fc2_ref,
    rows_ref,
    n1_ref,
    scale_ref,
    mix_ref,
    p_ref,
    o_ref,
    n2_ref,
    slope_ref,
    *rest,
):
    (grad_ref, send_ref, gy_ref, dab_ref, drb_ref, dmb_ref, sums_ref, table_ref) = rest[-10:-2]
    flat_ref, dob_ref = rest[-2:]
    slot = pl.program_id(0)

    @pl.when(slot == 0)
    def _():
        flat_ref[...] = jnp.zeros_like(flat_ref)

    load_image(returned_ref, cotangent_ref, info[1], flat_ref)
    alive = (slot < info[2]).astype(F32)
    upstream = nn(perm_ref[...], flat_ref[...]) * alive
    upstream_b = upstream.astype(BF)
    gy_ref[0, 0] = upstream_b
    sums_ref[0, 0, 12:16, :] = jnp.zeros((4, DIM), F32)
    sums_ref[0, 0, 7:8, :] = jnp.sum(upstream, axis=0, keepdims=True)
    grad_second = jnp.zeros((ROWS, DIM), F32)
    for chunk in range(CHUNKS):
        cols = slice(chunk * CHUNK, (chunk + 1) * CHUNK)
        grad_before = nt(upstream_b, fc2_ref[cols, :]) * slope_ref[0, 0, :, cols].astype(F32)
        sums_ref[0, 0, 8 + chunk : 9 + chunk, :] = jnp.sum(grad_before, axis=0, keepdims=True)
        grad_before_b = grad_before.astype(BF)
        dab_ref[0, 0, :, cols] = grad_before_b
        grad_second = grad_second + nt(grad_before_b, fc1_ref[:, cols])
    normed_b = n2_ref[0, 0].astype(F32)
    sums_ref[0, 0, 1:2, :] = jnp.sum(grad_second * normed_b, axis=0, keepdims=True)
    sums_ref[0, 0, 6:7, :] = jnp.sum(grad_second, axis=0, keepdims=True)
    grad_middle = upstream + norm_backward(
        grad_second * rows_ref[1:2, :], normed_b, scale_ref[0, 0, :, 128:129]
    )
    grad_middle_b = grad_middle.astype(BF)
    drb_ref[0, 0] = grad_middle_b
    sums_ref[0, 0, 5:6, :] = jnp.sum(grad_middle, axis=0, keepdims=True)
    dob_ref[...] = nt(grad_middle_b, proj_ref[...]).astype(BF)
    own = own_ref[...]
    own_f = own.astype(F32)
    match = match_ref[...]
    for window in range(PARTS):
        at = slice(window * SPAN, (window + 1) * SPAN)
        for group in range(GROUPS):
            feats = slice(group * FEAT, (group + 1) * FEAT)
            keys = slice(group * KEYS, (group + 1) * KEYS)
            query = mix_ref[0, 0, at, group * FEAT : (group + 1) * FEAT]
            key = mix_ref[0, 0, at, DIM + group * FEAT : DIM + (group + 1) * FEAT]
            value = mix_ref[0, 0, at, 2 * DIM + group * FEAT : 2 * DIM + (group + 1) * FEAT]
            probs = p_ref[0, 0, at, keys]
            grad_out = dob_ref[at, feats]
            grad_probs = nt(grad_out, spread_heads(value, own))
            level = grad_out.astype(F32) * o_ref[0, 0, at, feats].astype(F32)
            mean = nn(level.astype(BF), match)
            grad_scores = probs.astype(F32) * (grad_probs - mean)
            if window == 0:
                table_ref[0, 0, :, keys] = grad_scores
            else:
                table_ref[0, 0, :, keys] += grad_scores
            grad_scores_b = grad_scores.astype(BF)
            grad_query = nn(grad_scores_b, spread_heads(key, own)) * FACTOR
            grad_key = fold_heads(tn(grad_scores_b, query), own_f)
            grad_value = fold_heads(tn(probs, grad_out), own_f)
            dmb_ref[0, 0, at, group * FEAT : (group + 1) * FEAT] = grad_query.astype(BF)
            dmb_ref[0, 0, at, DIM + group * FEAT : DIM + (group + 1) * FEAT] = grad_key.astype(BF)
            dmb_ref[0, 0, at, 2 * DIM + group * FEAT : 2 * DIM + (group + 1) * FEAT] = grad_value.astype(BF)
            add_query = jnp.sum(grad_query, axis=0, keepdims=True)
            add_value = jnp.sum(grad_value, axis=0, keepdims=True)
            if window == 0:
                sums_ref[0, 0, 3:4, feats] = add_query
                sums_ref[0, 0, 4:5, feats] = add_value
            else:
                sums_ref[0, 0, 3:4, feats] += add_query
                sums_ref[0, 0, 4:5, feats] += add_value
    grad_first = nt(dmb_ref[0, 0], qkv_ref[...])
    normed_a = n1_ref[0, 0].astype(F32)
    sums_ref[0, 0, 0:1, :] = jnp.sum(grad_first * normed_a, axis=0, keepdims=True)
    sums_ref[0, 0, 2:3, :] = jnp.sum(grad_first, axis=0, keepdims=True)
    grad_rows = grad_middle + norm_backward(
        grad_first * rows_ref[0:1, :], normed_a, scale_ref[0, 0, :, 0:1]
    )
    image = nn(back_ref[...], grad_rows.astype(BF))
    image_b = image.astype(BF)
    for row in range(SIDE):
        grad_ref[0, 0, row] = image[row * LINE : row * LINE + SIDE]
        send_ref[0, 0, row] = image_b[row * LINE : row * LINE + SIDE]


def whole(array):
    rank = array.ndim
    return pl.BlockSpec(array.shape, lambda i, info: (0,) * rank, pipeline_mode=pl.Buffered(1))


def image_shape(lead, dtype):
    return jax.ShapeDtypeStruct(lead + (SIDE, SIDE, DIM), dtype)


def at_place(shape):
    tail = shape[2:]
    zeros = (0,) * len(tail)
    return pl.BlockSpec((1, 1) + tail, lambda i, info: (info[0], i) + zeros)


def at_slot(shape):
    tail = shape[2:]
    zeros = (0,) * len(tail)
    return pl.BlockSpec((1, 1) + tail, lambda i, info: (0, i) + zeros)


def run(kernel, info, ins, in_specs, outs, out_specs, stores, scratch, name, after=None):
    slots = outs[0].shape[1]
    aliases = {}
    args = [info] + list(ins)
    specs = list(in_specs)
    if stores is not None:
        for position, store in stores:
            aliases[len(args)] = position
            args.append(store)
            specs.append(pl.BlockSpec(memory_space=pl.ANY))
    if after is not None:
        args.append(after)
        specs.append(pl.BlockSpec(memory_space=pl.ANY))
    return pl.pallas_call(
        kernel,
        out_shape=outs,
        grid_spec=pltpu.PrefetchScalarGridSpec(
            num_scalar_prefetch=1,
            grid=(slots,),
            in_specs=specs,
            out_specs=out_specs,
            scratch_shapes=scratch,
        ),
        input_output_aliases=aliases,
        compiler_params=pltpu.CompilerParams(
            dimension_semantics=("arbitrary",), vmem_limit_bytes=58 << 20
        ),
        name=name,
    )(*args)


def token_places(offset):
    index = lax.broadcasted_iota(jnp.int32, (ROWS, FLAT), 0)
    window, inner = index // SPAN, index % SPAN
    line = (window // 2) * WIN + inner // WIN + offset
    column = (window % 2) * WIN + inner % WIN + offset
    line = jnp.where(line >= SIDE, line - SIDE, line)
    column = jnp.where(column >= SIDE, column - SIDE, column)
    return jnp.where(inner < AREA, line * LINE + column, -1)


def attention_add(table, relpos, regions, later):
    onehot = (relpos.reshape(AREA, AREA)[:, :, None] == jnp.arange(TABLE, dtype=jnp.int32)).astype(BF)
    lookup = lax.dot_general(onehot, table, (((2,), (0,)), ((), ())), preferred_element_type=F32)
    lookup = lookup.transpose(0, 2, 1)
    lookup = jnp.pad(
        lookup, ((0, SPAN - AREA), (0, 0), (0, SPAN - AREA)), constant_values=0.0
    )
    side = SIDE // WIN
    tiles = regions.reshape(side, WIN, side, WIN).transpose(0, 2, 1, 3).reshape(PARTS, AREA)
    tiles = jnp.pad(tiles, ((0, 0), (0, SPAN - AREA)))
    shape = (PARTS, SPAN, SPAN)
    present = lax.broadcasted_iota(jnp.int32, shape, 1) < AREA
    differ = (tiles[:, :, None] != tiles[:, None, :]) & later & present
    mask = jnp.where(differ, F32(-100.0), F32(0.0))
    absent = lax.broadcasted_iota(jnp.int32, shape, 2) >= AREA
    mask = jnp.where(absent, F32(NEVER), mask)
    return (lookup[None] + mask[:, :, None, :]).reshape(PARTS, SPAN, HEADS * SPAN)


def table_gradient(summed, relpos):
    pairs = summed.reshape(SPAN, HEADS, SPAN)[:AREA, :, :AREA]
    onehot = (relpos[:, :, None] == jnp.arange(TABLE, dtype=jnp.int32)).astype(F32)
    return lax.dot_general(
        onehot.reshape(AREA * AREA, TABLE),
        pairs.transpose(0, 2, 1).reshape(AREA * AREA, HEADS),
        (((0,), (0,)), ((), ())),
        precision=lax.Precision.HIGHEST,
        preferred_element_type=F32,
    )


def shifted(value, axis, by):
    length = lax.axis_size(axis)
    pairs = [(i, i + by) for i in range(length) if 0 <= i + by < length]
    return lax.ppermute(value, axis, pairs)


def shards(
    images,
    cotangent,
    counts,
    regions,
    relpos,
    qkv_weight,
    proj_weight,
    fc1_weight,
    fc2_weight,
    gains,
    biases,
    fc1_bias,
    rel_table,
):
    section = lax.axis_index("section")
    later = section == 1
    flag = later.astype(jnp.int32)
    micro, slots = images.shape[:2]
    pieces = lax.axis_size("fsdp")
    width = DIM // pieces

    small = jnp.concatenate(
        [gains[0].reshape(-1), biases[0].reshape(-1), fc1_bias[0].reshape(-1), rel_table[0].reshape(-1)]
    )
    small = jnp.pad(small, (0, -small.shape[0] % 1024)).reshape(-1, 128)
    small = lax.all_gather(small, "fsdp", axis=0, tiled=False).reshape(pieces, -1)
    qkv_w = lax.all_gather(qkv_weight[0], "fsdp", axis=0, tiled=True)
    proj_w = lax.all_gather(proj_weight[0], "fsdp", axis=0, tiled=True)
    fc1_w = lax.all_gather(fc1_weight[0], "fsdp", axis=0, tiled=True)
    fc2_w = lax.all_gather(fc2_weight[0], "fsdp", axis=0, tiled=True)
    cut_a, cut_b = 8 * width, 8 * width + HIDDEN // pieces
    rows = small[:, :cut_a].reshape(pieces, 8, width).transpose(1, 0, 2).reshape(8, DIM).astype(F32)
    hidden_bias = small[:, cut_a:cut_b].reshape(1, HIDDEN).astype(F32)
    per_piece = HEADS // pieces
    table = small[:, cut_b : cut_b + TABLE * per_piece].reshape(pieces, TABLE, per_piece)
    table = table.transpose(1, 0, 2).reshape(TABLE, HEADS)

    places = token_places(SHIFT * flag)
    perm = (places == lax.broadcasted_iota(jnp.int32, (ROWS, FLAT), 1)).astype(BF)
    back = perm.T
    added = attention_add(table, relpos, regions, later)
    key_head = lax.broadcasted_iota(jnp.int32, (KEYS, FEAT), 0) // SPAN
    own = (key_head == lax.broadcasted_iota(jnp.int32, (KEYS, FEAT), 1) // HEAD_DIM).astype(BF)
    match = own.T
    same = (
        lax.broadcasted_iota(jnp.int32, (KEYS, KEYS), 0) // SPAN
        == lax.broadcasted_iota(jnp.int32, (KEYS, KEYS), 1) // SPAN
    ).astype(BF)

    lead = (micro, slots)
    bank = lambda width, dtype=BF, rows=ROWS: jax.ShapeDtypeStruct(lead + (rows, width), dtype)
    small_lead = (1, slots)
    send_shape = image_shape(small_lead, BF)
    fwd_outs = (
        image_shape(lead, BF),
        send_shape,
        bank(DIM),
        bank(DIM),
        bank(256, F32),
        bank(3 * DIM),
        bank(HEADS * SPAN),
        bank(DIM),
        bank(DIM),
        bank(DIM),
        bank(HIDDEN),
        bank(HIDDEN),
    )
    bwd_outs = (
        image_shape(lead, F32),
        send_shape,
        bank(DIM),
        bank(HIDDEN),
        bank(DIM),
        bank(3 * DIM),
        bank(DIM, F32, SUMS),
        bank(HEADS * SPAN, F32, SPAN),
    )
    specs_of = lambda outs: tuple(
        at_slot(o.shape) if i == 1 else at_place(o.shape) for i, o in enumerate(outs)
    )
    weights = (qkv_w, proj_w, fc1_w, fc2_w)

    def describe(position):
        place = jnp.clip(position, 0, micro - 1)
        count = lax.dynamic_index_in_dim(counts[:, 0], place, 0, keepdims=False)
        return jnp.stack([place, flag, count]).astype(jnp.int32)

    def forward_step(position, carried, held, after):
        info = describe(position)
        consts = (perm, back, added, own, same) + weights + (rows, hidden_bias)
        ins = (images, carried) + consts
        in_specs = [at_place(images.shape), at_slot(carried.shape)] + [whole(c) for c in consts]
        stores = None if held is None else [(i, h) for i, h in enumerate(held) if i != 1]
        return run(
            forward_kernel, info, ins, in_specs, fwd_outs, specs_of(fwd_outs), stores,
            [pltpu.VMEM((FLAT, DIM), BF)], "forward", after,
        )

    def backward_step(position, returned, saved, held, after):
        info = describe(position)
        consts = (perm, back, own, match) + weights + (rows,)
        kept = (saved[2], saved[4], saved[5], saved[6], saved[7], saved[8], saved[11])
        ins = (cotangent, returned) + consts + kept
        in_specs = (
            [at_place(cotangent.shape), at_slot(returned.shape)]
            + [whole(c) for c in consts]
            + [at_place(k.shape) for k in kept]
        )
        stores = None if held is None else [(i, h) for i, h in enumerate(held) if i != 1]
        return run(
            backward_kernel, info, ins, in_specs, bwd_outs, specs_of(bwd_outs), stores,
            [pltpu.VMEM((FLAT, DIM), BF), pltpu.VMEM((ROWS, DIM), BF)], "backward", after,
        )

    carried = jnp.zeros(send_shape.shape, BF)
    returned = jnp.zeros(send_shape.shape, BF)
    saved = grads = None
    for moment in range(micro + 2):
        if moment <= micro:
            after = None if grads is None else grads[6]
            saved = forward_step(moment - flag, carried, saved, after)
            if moment < micro:
                carried = shifted(saved[1], "section", 1)
        if moment >= 1:
            grads = backward_step(moment - 2 + flag, returned, saved, grads, None)
            if moment <= micro:
                returned = shifted(grads[1], "section", -1)

    flat = lambda a: a.reshape(-1, a.shape[-1])
    h1, o, h2, u = (flat(saved[i]) for i in (3, 7, 9, 10))
    gy, dab, drb, dmb = (flat(grads[i]) for i in (2, 3, 4, 5))
    big = [tn(u, gy), tn(h2, dab), tn(h1, dmb), tn(o, drb)]
    big = [lax.psum_scatter(b.astype(BF), "fsdp", scatter_dimension=0, tiled=True) for b in big]
    big = [lax.psum(b, "replica").astype(F32)[None] for b in big]
    sums = jnp.sum(grads[6], axis=(0, 1))
    table_grad = table_gradient(jnp.sum(grads[7], axis=(0, 1)), relpos)
    spread = jnp.concatenate(
        [
            sums[:8].reshape(8, pieces, width).transpose(1, 0, 2).reshape(pieces, -1),
            sums[8:12].reshape(pieces, -1),
            table_grad.reshape(TABLE, pieces, per_piece).transpose(1, 0, 2).reshape(pieces, -1),
        ],
        axis=1,
    )
    spread = jnp.pad(spread, ((0, 0), (0, -spread.shape[1] % 1024)))
    total = lax.psum(lax.psum_scatter(spread, "fsdp", scatter_dimension=0, tiled=True), "replica")[0]
    vectors = total[:cut_a].reshape(8, width)
    return (
        saved[0][None],
        grads[0][None],
        big[2],
        big[3],
        big[1],
        big[0],
        vectors[None, :2],
        vectors[None, 2:],
        total[None, cut_a:cut_b],
        total[cut_b : cut_b + TABLE * per_piece].reshape(1, TABLE, per_piece),
    )


def solution(mesh):
    in_specs = (
        P(None, ("fsdp", "replica"), None, None, None),
        P(None, ("fsdp", "replica"), None, None, None),
        P(None, ("fsdp", "replica")),
        P(),
        P(),
        P("section", "fsdp", None),
        P("section", "fsdp", None),
        P("section", "fsdp", None),
        P("section", "fsdp", None),
        P("section", None, "fsdp"),
        P("section", None, "fsdp"),
        P("section", "fsdp"),
        P("section", None, "fsdp"),
    )
    out_specs = (
        P("section", None, ("fsdp", "replica"), None, None, None),
        P("section", None, ("fsdp", "replica"), None, None, None),
        P("section", "fsdp", None),
        P("section", "fsdp", None),
        P("section", "fsdp", None),
        P("section", "fsdp", None),
        P("section", None, "fsdp"),
        P("section", None, "fsdp"),
        P("section", "fsdp"),
        P("section", None, "fsdp"),
    )
    return jax.shard_map(shards, mesh=mesh, in_specs=in_specs, out_specs=out_specs, check_vma=False)
```

```python
import functools

import jax
import jax.numpy as jnp
from jax import lax
from jax.experimental import pallas as pl
from jax.experimental.pallas import tpu as pltpu
from jax.sharding import PartitionSpec as P

DIM = 512
HEADS = 16
HEAD_DIM = 32
HIDDEN = 2048
WIN = 7
SIDE = 14
SHIFT = 3
TABLE = 169

AREA = WIN * WIN
PARTS = (SIDE // WIN) ** 2
SPAN = 64
ROWS = PARTS * SPAN
LINE = 16
FLAT = SIDE * LINE
GROUP = 4
GROUPS = HEADS // GROUP
KEYS = GROUP * SPAN
FEAT = GROUP * HEAD_DIM
CHUNK = 512
CHUNKS = HIDDEN // CHUNK
SUMS = 16

EPSILON = 1e-05
ROOT_HALF = 0.7071067811865476
INV_ROOT_TAU = 0.3989422804014327
LOG2_E = 1.4426950408889634
FACTOR = HEAD_DIM ** (-0.5)
NEVER = -1e30


BF = jnp.bfloat16
F32 = jnp.float32


def nn(left, right):
    return lax.dot_general(left, right, (((1,), (0,)), ((), ())), preferred_element_type=F32)


def nt(left, right):
    return lax.dot_general(left, right, (((1,), (1,)), ((), ())), preferred_element_type=F32)


def tn(left, right):
    return lax.dot_general(left, right, (((0,), (0,)), ((), ())), preferred_element_type=F32)


def normalize(values):
    center = values - jnp.mean(values, axis=-1, keepdims=True)
    spread = jnp.mean(center * center, axis=-1, keepdims=True)
    scaled = lax.rsqrt(spread + EPSILON)
    return center * scaled, scaled


def norm_backward(direct, normed, scaled):
    return (
        direct
        - jnp.mean(direct, axis=-1, keepdims=True)
        - normed * jnp.mean(direct * normed, axis=-1, keepdims=True)
    ) * scaled


def fold_heads(stacked, own):
    kept = stacked * own
    total = kept[:SPAN]
    for head in range(1, GROUP):
        total = total + kept[head * SPAN : (head + 1) * SPAN]
    return total


def spread_heads(rows, own):
    return jnp.concatenate([rows] * GROUP, axis=0) * own


def pipeline(count, produce, consume):
    ready = produce(0)
    for k in range(count):
        following = produce(k + 1) if k + 1 < count else None
        consume(k, ready)
        ready = following


class Copies:
    def __init__(self, sems):
        self.sems = sems
        self.used = 0
        self.open = []

    def start(self, source, target):
        copy = pltpu.make_async_copy(source, target, self.sems.at[self.used])
        self.used += 1
        copy.start()
        return copy

    def store(self, source, target):
        self.open.append(self.start(source, target))

    def finish(self):
        for copy in self.open:
            copy.wait()


def fetch_group(copies, pieces, buffer, own):
    if len(pieces) == 1:
        return [copies.start(pieces[0], buffer)]
    started = []
    for j, piece in enumerate(pieces):
        rows = piece.shape[0]
        started.append(copies.start(piece, buffer.at[pl.ds(pl.multiple_of((own ^ j) * rows, rows), rows)]))
    return started


def arrived(started, buffer):
    for copy in started:
        copy.wait()
    return buffer


def fetch_image(copies, native, flat, place, use_native, native_buffer, flat_buffer):
    first, second = copies.sems.at[copies.used], copies.sems.at[copies.used + 1]
    copies.used += 2
    one = pltpu.make_async_copy(native.at[place], native_buffer, first)
    other = pltpu.make_async_copy(flat, flat_buffer, second)

    @pl.when(use_native)
    def _():
        one.start()

    @pl.when(jnp.logical_not(use_native))
    def _():
        other.start()

    def ready():
        @pl.when(use_native)
        def _():
            one.wait()
            edge = jnp.zeros((LINE - SIDE, DIM), BF)
            for slot in range(flat_buffer.shape[0]):
                for row in range(SIDE):
                    flat_buffer[slot, row * LINE : row * LINE + SIDE, :] = native_buffer[slot, row]
                    flat_buffer[slot, row * LINE + SIDE : (row + 1) * LINE, :] = edge

        @pl.when(jnp.logical_not(use_native))
        def _():
            other.wait()

    return ready


def forward_kernel(shape, slots, moment, info, perm_ref, back_ref, rows_ref, hidden_ref, *rest):
    images_ref, carried_ref = rest[:2]
    groups, rest = split_groups(rest[2:], shape)
    (
        send_ref, flat_ref, native_ref,
        n1_ref, h1_ref, scale_ref, mix_ref, p_ref, o_ref, n2_ref, h2_ref, u_ref, slope_ref,
    ) = rest[-14:-1]
    sems = rest[-1]
    buffers = rest[-14 - len(shape) : -14]
    outs = rest[-14 - len(shape) - 12 : -14 - len(shape)]
    rows = slots * ROWS
    windows = [slice(w * SPAN, (w + 1) * SPAN) for w in range(slots * PARTS)]
    later, own_place, place, count = info[0], info[1], info[2 + 2 * moment], info[3 + 2 * moment]
    copies = Copies(sems)
    image_ready = fetch_image(copies, images_ref, carried_ref, place, later == 0, native_ref, flat_ref)
    held = [fetch_group(copies, g, b, own_place) for g, b in zip(groups, buffers)]
    image_ready()
    base = jnp.concatenate([nn(perm_ref[...], flat_ref[slot]) for slot in range(slots)], axis=0)
    normed_a, scaled_a = normalize(base)
    n1_ref[...] = normed_a.astype(BF)
    first = (normed_a * rows_ref[0:1, :] + rows_ref[2:3, :]).astype(BF)
    h1_ref[...] = first
    scale_ref[:, 0:128] = jnp.broadcast_to(scaled_a, (rows, 128))
    copies.store(n1_ref, outs[2].at[place])
    copies.store(h1_ref, outs[3].at[place])
    qkv_ref = arrived(held[0], buffers[0])
    mix_ref[:, :DIM] = ((nn(first, qkv_ref[:, :DIM]) + rows_ref[3:4, :]) * FACTOR).astype(BF)
    mix_ref[:, DIM : 2 * DIM] = nn(first, qkv_ref[:, DIM : 2 * DIM]).astype(BF)
    mix_ref[:, 2 * DIM :] = (nn(first, qkv_ref[:, 2 * DIM :]) + rows_ref[4:5, :]).astype(BF)
    copies.store(mix_ref, outs[5].at[place])
    own = arrived(held[1], buffers[1])[...]
    added_ref = arrived(held[2], buffers[2])
    same = arrived(held[3], buffers[3])[...]

    def weigh(group):
        feats = slice(group * FEAT, (group + 1) * FEAT)
        keys = slice(group * KEYS, (group + 1) * KEYS)
        expo = []
        for index, at in enumerate(windows):
            key = mix_ref[at, DIM + feats.start : DIM + feats.stop]
            scores = nt(mix_ref[at, feats], spread_heads(key, own))
            expo.append(jnp.exp(scores + added_ref[index % PARTS, :, keys]))
        return jnp.concatenate(expo, axis=0)

    def attend(group, expo):
        feats = slice(group * FEAT, (group + 1) * FEAT)
        keys = slice(group * KEYS, (group + 1) * KEYS)
        probs = (expo / nn(expo.astype(BF), same)).astype(BF)
        p_ref[:, keys] = probs
        for at in windows:
            value = mix_ref[at, 2 * DIM + feats.start : 2 * DIM + feats.stop]
            o_ref[at, feats] = nn(probs[at], spread_heads(value, own)).astype(BF)

    pipeline(GROUPS, weigh, attend)
    copies.store(p_ref, outs[6].at[place])
    copies.store(o_ref, outs[7].at[place])
    proj_ref = arrived(held[4], buffers[4])
    middle = base + nn(o_ref[...], proj_ref[...]) + rows_ref[5:6, :]
    normed_b, scaled_b = normalize(middle)
    n2_ref[...] = normed_b.astype(BF)
    scale_ref[:, 128:256] = jnp.broadcast_to(scaled_b, (rows, 128))
    second = (normed_b * rows_ref[1:2, :] + rows_ref[6:7, :]).astype(BF)
    h2_ref[...] = second
    copies.store(n2_ref, outs[8].at[place])
    copies.store(h2_ref, outs[9].at[place])
    copies.store(scale_ref, outs[4].at[place])
    fc1_ref = arrived(held[5], buffers[5])
    fc2_ref = arrived(held[6], buffers[6])
    total = [middle + rows_ref[7:8, :]]

    def widen(chunk):
        cols = slice(chunk * CHUNK, (chunk + 1) * CHUNK)
        return nn(second, fc1_ref[:, cols]) + hidden_ref[0:1, cols]

    def narrow(chunk, before):
        cols = slice(chunk * CHUNK, (chunk + 1) * CHUNK)
        scaled = before * ROOT_HALF
        share = 0.5 + 0.5 * lax.erf(scaled)
        hidden = (before * share).astype(BF)
        u_ref[:, cols] = hidden
        bell = jnp.exp2(scaled * scaled * -LOG2_E)
        slope_ref[:, cols] = (share + (before * INV_ROOT_TAU) * bell).astype(BF)
        copies.store(u_ref.at[:, cols], outs[10].at[place, :, cols])
        copies.store(slope_ref.at[:, cols], outs[11].at[place, :, cols])
        total[0] = total[0] + nn(hidden, fc2_ref[cols, :])

    pipeline(CHUNKS, widen, narrow)
    output = total[0].astype(BF)
    for slot in range(slots):
        alive = (slot < count).astype(F32)
        image = (nn(back_ref[...], output[slot * ROWS : (slot + 1) * ROWS]) * alive).astype(BF)
        send_ref[slot] = image
        for row in range(SIDE):
            native_ref[slot, row] = image[row * LINE : row * LINE + SIDE]
    copies.store(send_ref, outs[1])
    copies.store(native_ref, outs[0].at[place])
    copies.finish()


def backward_kernel(shape, slots, moment, info, perm_ref, back_ref, rows_ref, *rest):
    cotangent_ref, returned_ref = rest[:2]
    kept = rest[2:9]
    groups, rest = split_groups(rest[9:], shape)
    (
        send_ref, flat_ref, native_ref, grad_ref, dob_ref,
        gy_ref, dab_ref, drb_ref, dmb_ref, sums_ref, table_ref,
        n1_ref, scale_ref, mix_ref, p_ref, o_ref, n2_ref, slope_ref,
    ) = rest[-19:-1]
    sems = rest[-1]
    buffers = rest[-19 - len(shape) : -19]
    outs = rest[-19 - len(shape) - 8 : -19 - len(shape)]
    rows = slots * ROWS
    windows = [slice(w * SPAN, (w + 1) * SPAN) for w in range(slots * PARTS)]
    later, own_place, place, count = info[0], info[1], info[2 + 2 * moment], info[3 + 2 * moment]
    copies = Copies(sems)
    image_ready = fetch_image(copies, cotangent_ref, returned_ref, place, later != 0, native_ref, flat_ref)
    got = lambda index, buffer: [copies.start(kept[index].at[place], buffer)]
    held = [fetch_group(copies, groups[0], buffers[0], own_place)]
    slope_got = got(6, slope_ref)
    held.append(fetch_group(copies, groups[1], buffers[1], own_place))
    n2_got, scale_got = got(5, n2_ref), got(1, scale_ref)
    held += [fetch_group(copies, groups[k], buffers[k], own_place) for k in (2, 3, 4)]
    o_got, p_got, mix_got = got(4, o_ref), got(3, p_ref), got(2, mix_ref)
    held.append(fetch_group(copies, groups[5], buffers[5], own_place))
    n1_got = got(0, n1_ref)
    image_ready()
    upstream_b = jnp.concatenate(
        [
            (nn(perm_ref[...], flat_ref[slot]) * (slot < count).astype(F32)).astype(BF)
            for slot in range(slots)
        ],
        axis=0,
    )
    upstream = upstream_b.astype(F32)
    gy_ref[...] = upstream_b
    copies.store(gy_ref, outs[2].at[place])
    sums_ref[12:16, :] = jnp.zeros((4, DIM), F32)
    sums_ref[7:8, :] = jnp.sum(upstream, axis=0, keepdims=True)
    fc2_ref = arrived(held[0], buffers[0])
    arrived(slope_got, slope_ref)
    fc1_ref = arrived(held[1], buffers[1])
    total = [None]

    def widen(chunk):
        return nt(upstream_b, fc2_ref[chunk * CHUNK : (chunk + 1) * CHUNK, :])

    def narrow(chunk, wide):
        cols = slice(chunk * CHUNK, (chunk + 1) * CHUNK)
        grad_before = wide * slope_ref[:, cols].astype(F32)
        sums_ref[8 + chunk : 9 + chunk, :] = jnp.sum(grad_before, axis=0, keepdims=True)
        grad_before_b = grad_before.astype(BF)
        dab_ref[:, cols] = grad_before_b
        copies.store(dab_ref.at[:, cols], outs[3].at[place, :, cols])
        part = nt(grad_before_b, fc1_ref[:, cols])
        total[0] = part if chunk == 0 else total[0] + part

    pipeline(CHUNKS, widen, narrow)
    grad_second = total[0]
    normed_b = arrived(n2_got, n2_ref)[...].astype(F32)
    arrived(scale_got, scale_ref)
    sums_ref[1:2, :] = jnp.sum(grad_second * normed_b, axis=0, keepdims=True)
    sums_ref[6:7, :] = jnp.sum(grad_second, axis=0, keepdims=True)
    grad_middle = upstream + norm_backward(
        grad_second * rows_ref[1:2, :], normed_b, scale_ref[:, 128:129]
    )
    grad_middle_b = grad_middle.astype(BF)
    drb_ref[...] = grad_middle_b
    copies.store(drb_ref, outs[4].at[place])
    sums_ref[5:6, :] = jnp.sum(grad_middle, axis=0, keepdims=True)
    proj_ref = arrived(held[2], buffers[2])
    dob_ref[...] = nt(grad_middle_b, proj_ref[...]).astype(BF)
    own = arrived(held[3], buffers[3])[...]
    own_f = own.astype(F32)
    match = arrived(held[4], buffers[4])[...]
    arrived(o_got, o_ref)
    arrived(p_got, p_ref)
    arrived(mix_got, mix_ref)

    def score(group):
        feats = slice(group * FEAT, (group + 1) * FEAT)
        keys = slice(group * KEYS, (group + 1) * KEYS)
        level = dob_ref[:, feats].astype(F32) * o_ref[:, feats].astype(F32)
        mean = nn(level.astype(BF), match)
        found = []
        table = 0.0
        for at in windows:
            value = mix_ref[at, 2 * DIM + feats.start : 2 * DIM + feats.stop]
            grad_probs = nt(dob_ref[at, feats], spread_heads(value, own))
            grad_scores = p_ref[at, keys].astype(F32) * (grad_probs - mean[at])
            table = table + grad_scores
            found.append(grad_scores.astype(BF))
        table_ref[:, keys] = table
        return found

    def spread(group, found):
        feats = slice(group * FEAT, (group + 1) * FEAT)
        keys = slice(group * KEYS, (group + 1) * KEYS)
        key_feats = slice(DIM + feats.start, DIM + feats.stop)
        value_feats = slice(2 * DIM + feats.start, 2 * DIM + feats.stop)
        add_query = add_value = 0.0
        for at, scores in zip(windows, found):
            grad_query = nn(scores, spread_heads(mix_ref[at, key_feats], own)) * FACTOR
            grad_key = fold_heads(tn(scores, mix_ref[at, feats]), own_f)
            grad_value = fold_heads(tn(p_ref[at, keys], dob_ref[at, feats]), own_f)
            dmb_ref[at, feats] = grad_query.astype(BF)
            dmb_ref[at, key_feats] = grad_key.astype(BF)
            dmb_ref[at, value_feats] = grad_value.astype(BF)
            add_query = add_query + grad_query
            add_value = add_value + grad_value
        sums_ref[3:4, feats] = jnp.sum(add_query, axis=0, keepdims=True)
        sums_ref[4:5, feats] = jnp.sum(add_value, axis=0, keepdims=True)

    pipeline(GROUPS, score, spread)
    copies.store(dmb_ref, outs[5].at[place])
    copies.store(table_ref, outs[7].at[place])
    qkv_ref = arrived(held[5], buffers[5])
    grad_first = nt(dmb_ref[...], qkv_ref[...])
    normed_a = arrived(n1_got, n1_ref)[...].astype(F32)
    sums_ref[0:1, :] = jnp.sum(grad_first * normed_a, axis=0, keepdims=True)
    sums_ref[2:3, :] = jnp.sum(grad_first, axis=0, keepdims=True)
    copies.store(sums_ref, outs[6].at[place])
    grad_rows = grad_middle + norm_backward(
        grad_first * rows_ref[0:1, :], normed_a, scale_ref[:, 0:1]
    )
    grad_rows = grad_rows.astype(BF)
    for slot in range(slots):
        image = nn(back_ref[...], grad_rows[slot * ROWS : (slot + 1) * ROWS])
        send_ref[slot] = image.astype(BF)
        for row in range(SIDE):
            grad_ref[slot, row] = image[row * LINE : row * LINE + SIDE]
    copies.store(send_ref, outs[1])
    copies.store(grad_ref, outs[0].at[place])
    copies.finish()


def split_groups(refs, shape):
    groups = []
    for count in shape:
        groups.append(refs[:count])
        refs = refs[count:]
    return groups, refs


def run(kernel, moment, slots, info, consts, ins, groups, outs, stores, scratch, name, after):
    anywhere = pl.BlockSpec(memory_space=pl.ANY)
    inside = pl.BlockSpec(memory_space=pltpu.VMEM)
    args = [info] + list(consts) + list(ins) + [piece for group in groups for piece in group]
    specs = [inside] * len(consts) + [anywhere] * (len(args) - 1 - len(consts))
    aliases = {}
    if stores is not None:
        for position, store in enumerate(stores):
            if position != 1:
                aliases[len(args)] = position
                args.append(store)
                specs.append(anywhere)
    if after is not None:
        args.append(after)
        specs.append(anywhere)
    buffers = []
    for group in groups:
        rows = sum(piece.shape[0] for piece in group)
        buffers.append(pltpu.VMEM((rows,) + group[0].shape[1:], group[0].dtype))
    shape = tuple(len(group) for group in groups)
    copies = 2 + sum(shape) + 7 + len(outs) + 2 * CHUNKS
    return pl.pallas_call(
        functools.partial(kernel, shape, slots, moment),
        out_shape=outs,
        grid_spec=pltpu.PrefetchScalarGridSpec(
            num_scalar_prefetch=1,
            grid=(),
            in_specs=specs,
            out_specs=tuple(anywhere for _ in outs),
            scratch_shapes=buffers + scratch + [pltpu.SemaphoreType.DMA((copies,))],
        ),
        input_output_aliases=aliases,
        compiler_params=pltpu.CompilerParams(vmem_limit_bytes=58 << 20),
        name=name,
    )(*args)


def token_places(offset):
    index = lax.broadcasted_iota(jnp.int32, (ROWS, FLAT), 0)
    window, inner = index // SPAN, index % SPAN
    line = (window // 2) * WIN + inner // WIN + offset
    column = (window % 2) * WIN + inner % WIN + offset
    line = jnp.where(line >= SIDE, line - SIDE, line)
    column = jnp.where(column >= SIDE, column - SIDE, column)
    return jnp.where(inner < AREA, line * LINE + column, -1)


def attention_add(table, relpos, regions, later):
    onehot = (relpos.reshape(AREA, AREA)[:, :, None] == jnp.arange(TABLE, dtype=jnp.int32)).astype(BF)
    lookup = lax.dot_general(onehot, table, (((2,), (0,)), ((), ())), preferred_element_type=F32)
    lookup = lookup.transpose(0, 2, 1)
    lookup = jnp.pad(
        lookup, ((0, SPAN - AREA), (0, 0), (0, SPAN - AREA)), constant_values=0.0
    )
    side = SIDE // WIN
    tiles = regions.reshape(side, WIN, side, WIN).transpose(0, 2, 1, 3).reshape(PARTS, AREA)
    tiles = jnp.pad(tiles, ((0, 0), (0, SPAN - AREA)))
    shape = (PARTS, SPAN, SPAN)
    present = lax.broadcasted_iota(jnp.int32, shape, 1) < AREA
    differ = (tiles[:, :, None] != tiles[:, None, :]) & later & present
    mask = jnp.where(differ, F32(-100.0), F32(0.0))
    absent = lax.broadcasted_iota(jnp.int32, shape, 2) >= AREA
    mask = jnp.where(absent, F32(NEVER), mask)
    return (lookup[None] + mask[:, :, None, :]).reshape(PARTS, SPAN, HEADS * SPAN)


def table_gradient(summed, relpos):
    pairs = summed.reshape(SPAN, HEADS, SPAN)[:AREA, :, :AREA]
    onehot = (relpos[:, :, None] == jnp.arange(TABLE, dtype=jnp.int32)).astype(F32)
    return lax.dot_general(
        onehot.reshape(AREA * AREA, TABLE),
        pairs.transpose(0, 2, 1).reshape(AREA * AREA, HEADS),
        (((0,), (0,)), ((), ())),
        precision=lax.Precision.HIGHEST,
        preferred_element_type=F32,
    )


def exchange(value, axis, bit):
    return lax.ppermute(value, axis, [(i, i ^ bit) for i in range(lax.axis_size(axis))])


def bits_of(size):
    assert size & (size - 1) == 0
    return [1 << k for k in range(size.bit_length() - 1)]


def gather_pieces(shard, axis):
    pieces = {0: shard}
    for bit in reversed(bits_of(lax.axis_size(axis))):
        pieces.update({j | bit: exchange(piece, axis, bit) for j, piece in list(pieces.items())})
    return [pieces[j] for j in range(len(pieces))]


def in_order(pieces, place):
    stacked = jnp.stack(pieces)
    for bit in bits_of(len(pieces)):
        parts = stacked.reshape(-1, 2, bit, *stacked.shape[1:])
        stacked = jnp.where((place & bit) != 0, parts[:, ::-1], parts).reshape(stacked.shape)
    return stacked


def take(parts, index, axis=0):
    return lax.dynamic_index_in_dim(parts, index, axis, keepdims=False)


def scatter_sum(parts, axis, place, kind):
    for bit in bits_of(lax.axis_size(axis)):
        pairs = parts.reshape(parts.shape[0] // 2, 2, *parts.shape[1:])
        mine = (place & bit) // bit
        sent = exchange(take(pairs, 1 - mine, 1).astype(kind), axis, bit)
        parts = take(pairs, mine, 1).astype(F32) + sent.astype(F32)
    return parts[0]


def all_sum(part, axis, place, kind):
    bits = bits_of(lax.axis_size(axis))
    for bit in bits:
        halves = part.reshape(2, part.shape[0] // 2, *part.shape[1:])
        mine = (place & bit) // bit
        sent = exchange(take(halves, 1 - mine).astype(kind), axis, bit)
        part = take(halves, mine).astype(F32) + sent.astype(F32)
    part = part.astype(kind)
    for bit in reversed(bits):
        other = exchange(part, axis, bit)
        upper = (place & bit) != 0
        part = jnp.where(upper, jnp.stack([other, part]), jnp.stack([part, other]))
        part = part.reshape(-1, *part.shape[2:])
    return part.astype(F32)


def whole_sum(part, axis):
    for bit in bits_of(lax.axis_size(axis)):
        part = part + exchange(part, axis, bit)
    return part


def shards(
    images,
    cotangent,
    counts,
    regions,
    relpos,
    qkv_weight,
    proj_weight,
    fc1_weight,
    fc2_weight,
    gains,
    biases,
    fc1_bias,
    rel_table,
):
    section = lax.axis_index("section")
    later = section == 1
    flag = later.astype(jnp.int32)
    place = lax.axis_index("fsdp").astype(jnp.int32)
    deep = lax.axis_index("replica").astype(jnp.int32)
    micro, slots = images.shape[:2]
    pieces = lax.axis_size("fsdp")
    width = DIM // pieces

    small = jnp.concatenate(
        [gains[0].reshape(-1), biases[0].reshape(-1), fc1_bias[0].reshape(-1), rel_table[0].reshape(-1)]
    )
    small = jnp.pad(small, (0, -small.shape[0] % 1024)).reshape(-1, 128)
    small = [small] + [exchange(small, "fsdp", bit) for bit in range(1, pieces)]
    qkv_w, proj_w, fc1_w, fc2_w = (
        gather_pieces(w[0], "fsdp") for w in (qkv_weight, proj_weight, fc1_weight, fc2_weight)
    )
    small = in_order(small, place).reshape(pieces, -1)
    cut_a, cut_b = 8 * width, 8 * width + HIDDEN // pieces
    rows = small[:, :cut_a].reshape(pieces, 8, width).transpose(1, 0, 2).reshape(8, DIM).astype(F32)
    hidden_bias = small[:, cut_a:cut_b].reshape(1, HIDDEN).astype(F32)
    per_piece = HEADS // pieces
    table = small[:, cut_b : cut_b + TABLE * per_piece].reshape(pieces, TABLE, per_piece)
    table = table.transpose(1, 0, 2).reshape(TABLE, HEADS)

    places = token_places(SHIFT * flag)
    perm = (places == lax.broadcasted_iota(jnp.int32, (ROWS, FLAT), 1)).astype(BF)
    back = perm.T
    added = attention_add(table, relpos, regions, later)
    key_head = lax.broadcasted_iota(jnp.int32, (KEYS, FEAT), 0) // SPAN
    own = (key_head == lax.broadcasted_iota(jnp.int32, (KEYS, FEAT), 1) // HEAD_DIM).astype(BF)
    match = own.T
    same = (
        lax.broadcasted_iota(jnp.int32, (KEYS, KEYS), 0) // SPAN
        == lax.broadcasted_iota(jnp.int32, (KEYS, KEYS), 1) // SPAN
    ).astype(BF)

    turns = jnp.arange(micro + 1, dtype=jnp.int32)
    spots = jnp.clip(jnp.concatenate([turns - flag, turns - 1 + flag]), 0, micro - 1)
    hit = spots[:, None] == jnp.arange(micro, dtype=jnp.int32)[None, :]
    alive = jnp.sum(jnp.where(hit, counts[:, 0][None, :], 0), axis=1)
    info = jnp.concatenate([jnp.stack([flag, place]), jnp.stack([spots, alive], axis=1).reshape(-1)])

    span = slots * ROWS
    bank = lambda width, dtype=BF, rows=span: jax.ShapeDtypeStruct((micro, rows, width), dtype)
    image_of = lambda dtype: jax.ShapeDtypeStruct((micro, slots, SIDE, SIDE, DIM), dtype)
    send_shape = jax.ShapeDtypeStruct((slots, FLAT, DIM), BF)
    fwd_outs = (
        image_of(BF),
        send_shape,
        bank(DIM),
        bank(DIM),
        bank(256, F32),
        bank(3 * DIM),
        bank(HEADS * SPAN),
        bank(DIM),
        bank(DIM),
        bank(DIM),
        bank(HIDDEN),
        bank(HIDDEN),
    )
    bwd_outs = (
        image_of(F32),
        send_shape,
        bank(DIM),
        bank(HIDDEN),
        bank(DIM),
        bank(3 * DIM),
        bank(DIM, F32, SUMS),
        bank(HEADS * SPAN, F32, SPAN),
    )
    scratch_of = lambda o: pltpu.VMEM(o.shape[1:], o.dtype)
    shared_scratch = [
        pltpu.VMEM((slots, FLAT, DIM), BF),
        pltpu.VMEM((slots, FLAT, DIM), BF),
        pltpu.VMEM((slots, SIDE, SIDE, DIM), BF),
    ]

    def forward_step(turn, carried, held, after):
        consts = (perm, back, rows, hidden_bias)
        groups = (qkv_w, [own], [added], [same], proj_w, fc1_w, fc2_w)
        scratch = shared_scratch + [scratch_of(o) for o in fwd_outs[2:]]
        return run(
            forward_kernel, turn, slots, info, consts, (images, carried), groups, fwd_outs, held,
            scratch, "forward", after,
        )

    def backward_step(turn, returned, saved, held):
        consts = (perm, back, rows)
        kept = (saved[2], saved[4], saved[5], saved[6], saved[7], saved[8], saved[11])
        groups = (fc2_w, fc1_w, proj_w, [own], [match], qkv_w)
        scratch = (
            shared_scratch
            + [scratch_of(bwd_outs[0]), pltpu.VMEM((span, DIM), BF)]
            + [scratch_of(o) for o in bwd_outs[2:]]
            + [scratch_of(k) for k in kept]
        )
        return run(
            backward_kernel, micro + 1 + turn, slots, info, consts, (cotangent, returned) + kept, groups,
            bwd_outs, held, scratch, "backward", None,
        )

    carried = jnp.zeros(send_shape.shape, BF)
    returned = jnp.zeros(send_shape.shape, BF)
    saved = grads = None
    for turn in range(micro + 2):
        if turn <= micro:
            saved = forward_step(turn, carried, saved, None if grads is None else grads[6])
            if turn < micro:
                carried = exchange(saved[1], "section", 1)
        if turn >= 1:
            grads = backward_step(turn - 1, returned, saved, grads)
            if turn <= micro:
                returned = exchange(grads[1], "section", 1)

    flat = lambda a: a.reshape(-1, a.shape[-1])
    h1, o, h2, u = (flat(saved[i]) for i in (3, 7, 9, 10))
    gy, dab, drb, dmb = (flat(grads[i]) for i in (2, 3, 4, 5))

    def weight_gradient(left, right):
        parts = tn(left, right).astype(BF).reshape(pieces, -1, right.shape[1])
        part = scatter_sum(parts, "fsdp", place, BF)
        return all_sum(part, "replica", deep, BF)[None]

    grad_proj = weight_gradient(o, drb)
    grad_fc2 = weight_gradient(u, gy)
    grad_fc1 = weight_gradient(h2, dab)
    grad_qkv = weight_gradient(h1, dmb)
    sums = jnp.sum(grads[6], axis=0)
    table_grad = table_gradient(jnp.sum(grads[7], axis=0), relpos)
    spread = jnp.concatenate(
        [
            sums[:8].reshape(8, pieces, width).transpose(1, 0, 2).reshape(pieces, -1),
            sums[8:12].reshape(pieces, -1),
            table_grad.reshape(TABLE, pieces, per_piece).transpose(1, 0, 2).reshape(pieces, -1),
        ],
        axis=1,
    )
    spread = jnp.pad(spread, ((0, 0), (0, -spread.shape[1] % 1024)))
    spread = spread.reshape(pieces, -1, 128)
    total = whole_sum(scatter_sum(spread, "fsdp", place, F32), "replica").reshape(-1)
    vectors = total[:cut_a].reshape(8, width)
    return (
        saved[0][None],
        grads[0][None],
        grad_qkv,
        grad_proj,
        grad_fc1,
        grad_fc2,
        vectors[None, :2],
        vectors[None, 2:],
        total[None, cut_a:cut_b],
        total[cut_b : cut_b + TABLE * per_piece].reshape(1, TABLE, per_piece),
    )


def solution(mesh):
    in_specs = (
        P(None, ("fsdp", "replica"), None, None, None),
        P(None, ("fsdp", "replica"), None, None, None),
        P(None, ("fsdp", "replica")),
        P(),
        P(),
        P("section", "fsdp", None),
        P("section", "fsdp", None),
        P("section", "fsdp", None),
        P("section", "fsdp", None),
        P("section", None, "fsdp"),
        P("section", None, "fsdp"),
        P("section", "fsdp"),
        P("section", None, "fsdp"),
    )
    out_specs = (
        P("section", None, ("fsdp", "replica"), None, None, None),
        P("section", None, ("fsdp", "replica"), None, None, None),
        P("section", "fsdp", None),
        P("section", "fsdp", None),
        P("section", "fsdp", None),
        P("section", "fsdp", None),
        P("section", None, "fsdp"),
        P("section", None, "fsdp"),
        P("section", "fsdp"),
        P("section", None, "fsdp"),
    )
    return jax.shard_map(shards, mesh=mesh, in_specs=in_specs, out_specs=out_specs, check_vma=False)
```
